32 devices in a mesh: aux: 8 (over z, x), occ: 4 (over y, core).
Axes of the slice: x: 2, y: 2, z: 4, core: 2. Of those that a mesh axis runs over, the one named last changes fastest.
Arguments:
- blocks: float32 [384, 8, 4096], P('aux', 'occ'), may hold values from -6 to 6
- pair_list: int32 [8, 8, 2], P('aux', 'occ'), may hold values from 0 to 15
- pair_count: int32 [8], P('aux'), may hold values from 2 to 8, as said below
- orbitals: float32 [128, 1024], replicated, may hold values from -0.001953125 to 0.001953125
Outputs:
- exchange: float32 [1024, 1024], P('aux', 'occ')
The draws below stay inside these ranges and needn't reach their ends.
Inputs may be any that keep to these rules, and one draw needn't show every extreme that they name: `pair_list`: block indices of the kept pairs; pairs may repeat. `pair_count`: slots at or beyond an auxiliary block's count are padding and contribute nothing; some auxiliary block uses all 8 slots.
All inputs are finite; a program needn't handle non-finite values.
Results may differ from the reference program's by a relative error of at most 0.0003.
Values sent between devices are 32-bit elements; how exact they have to be, the bound alone decides.
A program may use at most 64 MiB of HBM per device.

```python
import jax
import jax.numpy as jnp
from jax import lax

NBF = 1024
BLK = 64
NOCC = 128
AUX_DEV = 48
NB = 16
KEPT = 8
NAUX = 384
N_AUX = 8


def draw_pair_count(key, part):
    counts = jax.random.randint(key, (N_AUX,), KEPT // 4, KEPT + 1).astype(jnp.int32)
    position = jax.random.randint(jax.random.fold_in(key, 7), (), 0, N_AUX)
    return counts.at[position].set(KEPT).astype(jnp.int32)


def place_ends(drawn, own_key, smallest, high):
    longest = drawn.shape.index(max(drawn.shape))
    spots = []
    for shift in (0, 1):
        where = [jax.random.randint(jax.random.fold_in(own_key, axis), (), 0, length) for axis, length in enumerate(drawn.shape)]
        where[longest] = (where[longest] + shift) % drawn.shape[longest]
        spots.append(tuple(where))
    return drawn.at[spots[0]].set(smallest).at[spots[1]].set(high)


def block_scale(key, shape, pieces, least, high):
    loudness, own = 1.0, jax.random.fold_in(key, 6)
    for dim, blocks in pieces:
        steps = jnp.exp(jax.random.uniform(jax.random.fold_in(own, dim), (blocks,), jnp.float32, least / len(pieces), high / len(pieces)))
        loudness = loudness * jnp.repeat(steps, shape[dim] // blocks).reshape([-1 if axis == dim else 1 for axis in range(len(shape))])
    return loudness


def scatter_about(key, dims, deviation, limit, pieces=(), kind=jnp.bfloat16):
    entries = deviation * jax.random.normal(key, dims, jnp.float32)
    if pieces:
        entries = entries * block_scale(key, dims, pieces, -0.22, 0.18)
    return jnp.clip(entries, -limit, limit).astype(kind)


def setup_inputs(seed: int = 0) -> dict:
    key_of = jax.random.split(jax.random.key(seed), 5)
    blocks = scatter_about(key_of[0], (NAUX, KEPT, BLK * BLK), 1.0, 6.0, ((0, 8), (1, 4)), jnp.float32)
    pair_list = place_ends(jax.random.randint(key_of[1], (N_AUX, KEPT, 2), 0, NB), jax.random.fold_in(key_of[1], 1), 0, NB - 1).astype(jnp.int32)
    pair_count = draw_pair_count(jax.random.fold_in(key_of[4], 71), 0)
    orbitals = scatter_about(key_of[3], (NOCC, NBF), (160 * AUX_DEV * N_AUX * NOCC) ** -0.5, 0.001953125, (), jnp.float32)
    return {"blocks": blocks, "pair_list": pair_list, "pair_count": pair_count, "orbitals": orbitals}


def reference(blocks, pair_list, pair_count, orbitals):
    n_blocks = NBF // BLK
    coefficients = orbitals.reshape(NOCC, n_blocks, BLK)
    tile_data = blocks.reshape(N_AUX, AUX_DEV, KEPT, BLK, BLK)
    positions = jnp.arange(n_blocks, dtype=jnp.int32)
    slot_index = jnp.arange(KEPT, dtype=jnp.int32)

    def one_block(total, inputs):
        tiles_here, pairs_here, count_here = inputs
        live_slot = slot_index < count_here
        row_onehot = ((pairs_here[:, 0][:, None] == positions[None, :]) & live_slot[:, None]).astype(jnp.float32)
        col_onehot = (pairs_here[:, 1][:, None] == positions[None, :]).astype(jnp.float32)
        picked_cols = jnp.einsum('iNn,sN->sin', coefficients, col_onehot, precision=lax.Precision.HIGHEST)
        half_tiles = jnp.einsum('qsmn,sin->isqm', tiles_here, picked_cols, precision=lax.Precision.HIGHEST)
        transformed = jnp.einsum('isqm,sM->iqMm', half_tiles, row_onehot, precision=lax.Precision.HIGHEST)
        transformed = transformed.reshape(NOCC * AUX_DEV, NBF)
        partial_value = jnp.einsum('rm,rn->mn', transformed, transformed, precision=lax.Precision.HIGHEST)
        return total + partial_value, None

    total, _ = lax.scan(one_block, jnp.zeros((NBF, NBF), jnp.float32), (tile_data, pair_list, pair_count))
    return total
```

```python
import functools

import jax
import jax.numpy as jnp
from jax import lax
from jax.experimental import pallas as pl
from jax.experimental.pallas import tpu as pltpu
from jax.sharding import PartitionSpec as P

LANES = 128
SIDE = 256
MESH = pl.DeviceIdType.MESH
NT = (((1,), (1,)), ((), ()))
NN = (((1,), (0,)), ((), ()))


def dot(a, b, dims):
    return lax.dot_general(a, b, dims, preferred_element_type=jnp.float32)


def split(x):
    hi = x.astype(jnp.bfloat16)
    return hi, (x - hi.astype(jnp.float32)).astype(jnp.bfloat16)


def kernel(n_aux, n_occ, n_sub, tiles, info, orb, out, rx, ids, whi, wlo, hhi, hlo, part, core_in,
           pair, y_in, full, dense, z_in, local_sem, tile_s, tile_r, ids_s, ids_r, idx_s, idx_r,
           core_s, core_r, ys_s, ys_r, gy_s, gy_r, gx_s, gx_r, fy_s, fy_r, gc_s, gc_r, z_s, z_r):
    a, o = lax.axis_index("aux"), lax.axis_index("occ")
    n_y, n_hi = n_occ // 2, n_aux // 2
    y, c = o // 2, lax.rem(o, 2)
    hi_a, lo = a // 2, lax.rem(a, 2)
    own_q = tiles.shape[0] // n_occ
    sub_q = own_q // n_sub
    krows = tiles.shape[1] // 2
    n_slots = 2 * n_occ
    n_side = n_slots * 2 * krows // SIDE
    total_rows = part.shape[0]
    half_rows, quarter = total_rows // 2, total_rows // n_occ

    def occ_peer(dy, dc):
        return lax.rem(y + dy, n_y) * 2 + (c if dc == 0 else 1 - c)

    peers = [(dy, dc) for dy in range(1, n_y) for dc in (0, 1)] + [(0, 1)]
    partner = (a, occ_peer(0, 1))
    x_peer = (a + 1 - 2 * lo, o)

    def z_peer(d):
        return (lax.rem(hi_a + d, n_hi) * 2 + lo, o)

    barrier = pltpu.get_barrier_semaphore()
    greet = [(a, occ_peer(*d)) for d in peers] + [x_peer] + [z_peer(d) for d in range(1, n_hi)]
    for dev in greet:
        pl.semaphore_signal(barrier, inc=1, device_id=dev, device_id_type=MESH)
    ids[lo, o] = info[...]
    own = pltpu.make_async_copy(tiles.at[pl.ds(o * own_q, own_q)], rx.at[o], local_sem)
    own.start()
    pl.semaphore_wait(barrier, len(greet))

    def remote(src, dst, s, r, dev):
        cp = pltpu.make_async_remote_copy(
            src_ref=src, dst_ref=dst, send_sem=s, recv_sem=r, device_id=dev, device_id_type=MESH
        )
        cp.start()
        return cp

    id_copies = []
    for d, (dy, dc) in enumerate(peers):
        id_copies.append(remote(info, ids.at[lo, o], ids_s.at[d], ids_r.at[d], (a, occ_peer(dy, dc))))
    tile_copies = []
    for j in range(n_sub):
        row = []
        for d, (dy, dc) in enumerate(peers):
            peer = occ_peer(dy, dc)
            row.append(remote(
                tiles.at[pl.ds(peer * own_q + j * sub_q, sub_q)],
                rx.at[o, pl.ds(j * sub_q, sub_q)],
                tile_s.at[j, d], tile_r.at[j, d], (a, peer)))
        tile_copies.append(row)
    for cp in id_copies:
        cp.wait()
    idx_copy = remote(ids.at[lo], ids.at[lo], idx_s, idx_r, x_peer)

    nbf, n_orb = orb.shape[1], orb.shape[0]
    orb_hi, orb_lo = split(orb[...])
    row_pos = lax.broadcasted_iota(jnp.int32, (nbf, LANES), 0)
    lane = lax.broadcasted_iota(jnp.int32, (n_orb, LANES), 1)
    for s in range(n_slots):
        sel = (row_pos == ids[lo, s // 2, pl.ds(s % 2, 1), :]).astype(jnp.float32).astype(jnp.bfloat16)
        for src, dst in ((orb_hi, whi), (orb_lo, wlo)):
            w = dot(src, sel, NN)
            dst[s, 0:n_orb, :] = jnp.where(lane < LANES // 2, w, 0.0).astype(jnp.bfloat16)
            dst[s, n_orb:2 * n_orb, :] = jnp.where(lane >= LANES // 2, w, 0.0).astype(jnp.bfloat16)

    own.wait()
    pairs = [(i, j) for i in range(n_side) for j in range(i + 1)]
    for j in range(n_sub):
        for cp in tile_copies[j]:
            cp.wait()
        for s in range(n_slots):
            rows = jnp.concatenate(
                [rx[s // 2, j * sub_q + q, pl.ds(s % 2, krows, stride=2), :] for q in range(sub_q)], axis=0)
            bh, bl = split(rows)
            res = dot(bh, whi[s], NT) + dot(bl, whi[s], NT) + dot(bh, wlo[s], NT)
            for q in range(sub_q):
                for p in range(2):
                    piece = res[q * krows:(q + 1) * krows, p * n_orb:(p + 1) * n_orb]
                    ph, pl_ = split(piece)
                    r0 = (2 * s + p) * krows
                    hhi[r0:r0 + krows, q * n_orb:(q + 1) * n_orb] = ph
                    hlo[r0:r0 + krows, q * n_orb:(q + 1) * n_orb] = pl_
        for b, (i, k) in enumerate(pairs):
            ih, il = hhi[i * SIDE:(i + 1) * SIDE, :], hlo[i * SIDE:(i + 1) * SIDE, :]
            kh, kl = hhi[k * SIDE:(k + 1) * SIDE, :], hlo[k * SIDE:(k + 1) * SIDE, :]
            val = dot(ih, kh, NT) + dot(ih, kl, NT) + dot(il, kh, NT)
            if j:
                val = val + part[b * SIDE:(b + 1) * SIDE, :]
            part[b * SIDE:(b + 1) * SIDE, :] = val

    cp = remote(part.at[pl.ds((1 - c) * half_rows, half_rows)], core_in, core_s, core_r, partner)
    cp.wait()
    pair[...] = part[pl.ds(pl.multiple_of(c * half_rows, 8), half_rows), :] + core_in[...]
    copies = []
    for d in range(1, n_y):
        dev_y = lax.rem(y + d, n_y)
        copies.append(remote(pair.at[pl.ds(dev_y * quarter, quarter)], y_in.at[d - 1],
                             ys_s.at[d - 1], ys_r.at[d - 1], (a, dev_y * 2 + c)))
    total = pair[pl.ds(pl.multiple_of(y * quarter, 8), quarter), :]
    for d in range(1, n_y):
        copies[d - 1].wait()
        total = total + y_in[d - 1]
    at = o_row = c * half_rows + y * quarter
    full[lo, pl.ds(pl.multiple_of(at, 8), quarter), :] = total
    mine = full.at[lo, pl.ds(o_row, quarter)]
    gx = remote(mine, mine, gx_s, gx_r, x_peer)
    gys = []
    for d in range(1, n_y):
        gys.append(remote(mine, mine, gy_s.at[d - 1], gy_r.at[d - 1],
                          (a, lax.rem(y + d, n_y) * 2 + c)))
    gx.wait()
    other = full.at[1 - lo, pl.ds(o_row, quarter)]
    fys = []
    for d in range(1, n_y):
        fys.append(remote(other, other, fy_s.at[d - 1], fy_r.at[d - 1],
                          (a, lax.rem(y + d, n_y) * 2 + c)))
    for cp in gys:
        cp.wait()
    mine_half = full.at[lo, pl.ds(c * half_rows, half_rows)]
    gc0 = remote(mine_half, mine_half, gc_s.at[0], gc_r.at[0], partner)
    for cp in fys:
        cp.wait()
    other_half = full.at[1 - lo, pl.ds(c * half_rows, half_rows)]
    gc1 = remote(other_half, other_half, gc_s.at[1], gc_r.at[1], partner)
    idx_copy.wait()
    gc0.wait()
    gc1.wait()

    out_rows, out_cols = out.shape
    compact = n_slots * 2 * krows
    col_pos = lax.broadcasted_iota(jnp.int32, (out_cols, compact), 0) + o * out_cols
    row_i = lax.broadcasted_iota(jnp.int32, (n_hi * out_rows, compact), 0)
    row_pos = (row_i // out_rows * 2 + lo) * out_rows + lax.rem(row_i, out_rows)
    acc = None
    for l in range(2):
        where = jnp.concatenate([ids[l, s, 2:3, :] for s in range(n_occ)], axis=1)
        cols = (col_pos == where).astype(jnp.float32).astype(jnp.bfloat16)
        rows = (row_pos == where).astype(jnp.float32).astype(jnp.bfloat16)
        t = [None] * n_side

        def add(i, v):
            t[i] = v if t[i] is None else t[i] + v

        for b, (i, k) in enumerate(pairs):
            for e in split(full[l, b * SIDE:(b + 1) * SIDE, :]):
                add(i, dot(e, cols[:, k * SIDE:(k + 1) * SIDE], NT))
                if i != k:
                    add(k, lax.dot_general(e, cols[:, i * SIDE:(i + 1) * SIDE], (((0,), (1,)), ((), ())),
                                           preferred_element_type=jnp.float32))
        for i in range(n_side):
            for e in split(t[i]):
                v = dot(rows[:, i * SIDE:(i + 1) * SIDE], e, NN)
                acc = v if acc is None else acc + v
    for h in range(n_hi):
        dense[h] = acc[h * out_rows:(h + 1) * out_rows, :]
    zs = []
    for d in range(1, n_hi):
        zs.append(remote(dense.at[lax.rem(hi_a + d, n_hi)], z_in.at[d - 1],
                         z_s.at[d - 1], z_r.at[d - 1], z_peer(d)))
    result = dense[hi_a]
    for d in range(1, n_hi):
        zs[d - 1].wait()
        result = result + z_in[d - 1]
    out[...] = result


def per_device(n_aux, n_occ, blocks, pair_list, pair_count, orbitals):
    n_q, slots, area = blocks.shape
    n_orb, nbf = orbitals.shape
    krows = area // LANES
    blk = LANES // 2
    tiles = blocks.reshape(n_q, slots, krows, LANES).transpose(0, 2, 1, 3).reshape(n_q, krows * slots, LANES)
    first = lax.axis_index("occ") * slots
    live = first + jnp.arange(slots, dtype=jnp.int32) < pair_count[0]
    lane = jnp.arange(LANES, dtype=jnp.int32)
    col_of = pair_list[0, :, 1][:, None] * blk + (lane % blk)[None, :]
    in_row = jnp.arange(blk, dtype=jnp.int32)
    in_row = in_row % krows * 2 + in_row // krows
    row_of = jnp.where(live[:, None], pair_list[0, :, 0][:, None] * blk + in_row[None, :], -1)
    info = jnp.concatenate([col_of, row_of.reshape(1, slots * blk), jnp.zeros((5, LANES), jnp.int32)], axis=0)

    own_q = n_q // n_occ
    n_sub = 3
    compact = slots * n_occ * blk
    n_side = compact // SIDE
    total_rows = n_side * (n_side + 1) // 2 * SIDE
    half, quarter = total_rows // 2, total_rows // n_occ
    n_y, n_hi = n_occ // 2, n_aux // 2
    out_rows, out_cols = nbf // n_aux, nbf // n_occ
    f32, bf16, dma = jnp.float32, jnp.bfloat16, pltpu.SemaphoreType.DMA
    return pl.pallas_call(
        functools.partial(kernel, n_aux, n_occ, n_sub),
        name="exchange",
        out_shape=jax.ShapeDtypeStruct((out_rows, out_cols), f32),
        in_specs=[pl.BlockSpec(memory_space=pl.ANY)] + [pl.BlockSpec(memory_space=pltpu.VMEM)] * 2,
        out_specs=pl.BlockSpec(memory_space=pltpu.VMEM),
        scratch_shapes=[
            pltpu.VMEM((n_occ, own_q, krows * slots, LANES), f32),
            pltpu.VMEM((2, n_occ, 8, LANES), jnp.int32),
            pltpu.VMEM((slots * n_occ, 2 * n_orb, LANES), bf16),
            pltpu.VMEM((slots * n_occ, 2 * n_orb, LANES), bf16),
            pltpu.VMEM((compact, own_q // n_sub * n_orb), bf16),
            pltpu.VMEM((compact, own_q // n_sub * n_orb), bf16),
            pltpu.VMEM((total_rows, SIDE), f32),
            pltpu.VMEM((half, SIDE), f32),
            pltpu.VMEM((half, SIDE), f32),
            pltpu.VMEM((n_y - 1, quarter, SIDE), f32),
            pltpu.VMEM((2, total_rows, SIDE), f32),
            pltpu.VMEM((n_hi, out_rows, out_cols), f32),
            pltpu.VMEM((n_hi - 1, out_rows, out_cols), f32),
            dma,
            dma((n_sub, n_occ - 1)), dma((n_sub, n_occ - 1)),
            dma((n_occ - 1,)), dma((n_occ - 1,)),
            dma, dma,
            dma, dma,
            dma((n_y - 1,)), dma((n_y - 1,)),
            dma((n_y - 1,)), dma((n_y - 1,)),
            dma, dma,
            dma((n_y - 1,)), dma((n_y - 1,)),
            dma((2,)), dma((2,)),
            dma((n_hi - 1,)), dma((n_hi - 1,)),
        ],
        compiler_params=pltpu.CompilerParams(collective_id=0, has_side_effects=True),
    )(tiles, info, orbitals)


def solution(mesh):
    body = functools.partial(per_device, mesh.shape["aux"], mesh.shape["occ"])
    in_specs = (P("aux", "occ", None), P("aux", "occ", None), P("aux"), P())
    return jax.shard_map(body, mesh=mesh, in_specs=in_specs, out_specs=P("aux", "occ"), check_vma=False)
```

```python
import functools

import jax
import jax.numpy as jnp
from jax import lax
from jax.experimental import pallas as pl
from jax.experimental.pallas import tpu as pltpu
from jax.sharding import PartitionSpec as P

LANES = 128
PIECES = 2
MESH = pl.DeviceIdType.MESH
NT = (((1,), (1,)), ((), ()))
NN = (((1,), (0,)), ((), ()))


def dot(a, b, dims):
    return lax.dot_general(a, b, dims, preferred_element_type=jnp.float32)


def split(x):
    hi = x.astype(jnp.bfloat16)
    return hi, (x - hi.astype(jnp.float32)).astype(jnp.bfloat16)


def kernel(n_aux, n_occ, n_sub, tiles, pairs_in, count_in, orb, out, rx, rxd, ids, whi, wlo, hhi, hlo,
           dhi, dlo, diag, dcore, dfull, off, ocore, opair, oin, ofull, dense, z_in,
           local_s, tile_s, tile_r, quart_s, quart_r, ids_s, ids_r, idx_s, idx_r, dc_s, dc_r,
           dx_s, dx_r, dy_s, dy_r, df_s, df_r, dd_s, dd_r, oc_s, oc_r, oy_s, oy_r, ox_s, ox_r,
           op_s, op_r, of_s, of_r, z_s, z_r):
    a, o = lax.axis_index("aux"), lax.axis_index("occ")
    n_y, n_hi = n_occ // 2, n_aux // 2
    y, c = o // 2, lax.rem(o, 2)
    hi_a, lo = a // 2, lax.rem(a, 2)
    own_q = tiles.shape[0] // n_occ
    sub_q = own_q // n_sub
    krows = tiles.shape[1] // 2
    blk = 2 * krows
    side = 4 * blk
    n_slots = 2 * n_occ
    n_off = n_y * (n_y - 1) // 2
    d_half, o_half = side // 2, n_off * side // 2
    piece = o_half // PIECES
    nbf, n_orb = orb.shape[1], orb.shape[0]

    def y_peer(d):
        return lax.rem(y + d, n_y)

    peers = [(d, e) for d in range(1, n_y) for e in (0, 1)] + [(0, 1)]

    def occ_peer(d, e):
        return y_peer(d) * 2 + (c if e == 0 else 1 - c)

    partner = (a, occ_peer(0, 1))
    x_peer = (a + 1 - 2 * lo, o)

    def z_peer(d):
        return (lax.rem(hi_a + d, n_hi) * 2 + lo, o)

    barrier = pltpu.get_barrier_semaphore()
    greet = [(a, occ_peer(*d)) for d in peers] + [x_peer] + [z_peer(d) for d in range(1, n_hi)]
    for dev in greet:
        pl.semaphore_signal(barrier, inc=1, device_id=dev, device_id_type=MESH)

    def local(src, dst, s):
        cp = pltpu.make_async_copy(src, dst, s)
        cp.start()
        return cp

    def quarter(index):
        return tiles.at[pl.ds(index * own_q, own_q)]

    locals_ = [local(quarter(o), rx.at[o], local_s.at[0])]
    for d in range(1, n_y):
        locals_.append(local(quarter(y_peer(d) * 2 + c), rxd.at[c, d - 1], local_s.at[d]))
    lane1 = lax.broadcasted_iota(jnp.int32, (8, LANES), 1)
    row1 = lax.broadcasted_iota(jnp.int32, (8, LANES), 0)
    within = lax.rem(lane1, blk)
    place = lax.rem(within, krows) * 2 + within // krows
    live = [jnp.where(o * 2 + s < count_in[0], pairs_in[0, s, 0] * blk, -nbf - blk) for s in range(2)]
    cols = jnp.where(row1 == 0, pairs_in[0, 0, 1], pairs_in[0, 1, 1]) * blk + within
    ids[lo, o] = jnp.where(row1 < 2, cols, jnp.where(lane1 < blk, live[0], live[1]) + place)
    pl.semaphore_wait(barrier, len(greet))

    def remote(src, dst, s, r, dev):
        cp = pltpu.make_async_remote_copy(
            src_ref=src, dst_ref=dst, send_sem=s, recv_sem=r, device_id=dev, device_id_type=MESH
        )
        cp.start()
        return cp

    def sub_tiles(j, d, e):
        peer = occ_peer(d, e)
        n = d * 2 + e
        return remote(tiles.at[pl.ds(peer * own_q + j * sub_q, sub_q)], rx.at[o, pl.ds(j * sub_q, sub_q)],
                      tile_s.at[j, n], tile_r.at[j, n], (a, peer))

    id_copies = []
    for n, d in enumerate(peers):
        id_copies.append(remote(ids.at[lo, o], ids.at[lo, o], ids_s.at[n], ids_r.at[n], (a, occ_peer(*d))))
    tile_copies = [[sub_tiles(j, d, e) for d in range(1, n_y) for e in (0, 1)] for j in range(n_sub)]
    quarters = []
    for d in range(1, n_y):
        quarters.append(remote(quarter(y_peer(d) * 2 + 1 - c), rxd.at[c, d - 1],
                               quart_s.at[d], quart_r.at[d], partner))
    quarters.append(remote(quarter(o + 1 - 2 * c), rx.at[o], quart_s.at[0], quart_r.at[0], partner))

    orb_hi, orb_lo = split(orb[...])
    row_pos = lax.broadcasted_iota(jnp.int32, (nbf, LANES), 0)
    lane = lax.broadcasted_iota(jnp.int32, (n_orb, LANES), 1)
    for cp in id_copies:
        cp.wait()
    idx_copy = remote(ids.at[lo], ids.at[lo], idx_s, idx_r, x_peer)
    for s in range(n_slots):
        sel = (row_pos == ids[lo, s // 2, pl.ds(s % 2, 1), :]).astype(jnp.float32)
        sel = sel.astype(jnp.bfloat16)
        for src, dst in ((orb_hi, whi), (orb_lo, wlo)):
            w = dot(src, sel, NN)
            dst[s, 0:n_orb, :] = jnp.where(lane < blk, w, 0.0).astype(jnp.bfloat16)
            dst[s, n_orb:2 * n_orb, :] = jnp.where(lane >= blk, w, 0.0).astype(jnp.bfloat16)

    def half(load, slot, row0, q0, hi_ref, lo_ref):
        rows = jnp.concatenate([load(q) for q in range(sub_q)], axis=0)
        bh, bl = split(rows)
        wh, wl = whi[slot], wlo[slot]
        res = dot(bh, wh, NT) + dot(bl, wh, NT) + dot(bh, wl, NT)
        for q in range(sub_q):
            for p in range(2):
                ph, pl_ = split(res[q * krows:(q + 1) * krows, p * n_orb:(p + 1) * n_orb])
                at = pl.ds(pl.multiple_of(row0 + p * krows, krows), krows)
                lanes = slice((q0 + q) * n_orb, (q0 + q + 1) * n_orb)
                hi_ref[at, lanes] = ph
                lo_ref[at, lanes] = pl_

    def gram(hi_i, lo_i, hi_k, lo_k):
        return dot(hi_i, hi_k, NT) + dot(hi_i, lo_k, NT) + dot(lo_i, hi_k, NT)

    for cp in locals_ + quarters:
        cp.wait()
    total = None
    for d in range(1, n_y):
        for j in range(n_sub):
            for e in range(2):
                for s in range(2):
                    half(lambda q: rxd[e, d - 1, j * sub_q + q, pl.ds(s, krows, stride=2), :],
                         (y * 2 + e) * 2 + s, (e * 2 + s) * blk, 0, dhi, dlo)
            val = gram(dhi[...], dlo[...], dhi[...], dlo[...])
            total = val if total is None else total + val
    mine = pl.ds(pl.multiple_of(y * side, side), side)
    for j in range(n_sub):
        for e in range(2):
            for s in range(2):
                half(lambda q: rx[y * 2 + e, j * sub_q + q, pl.ds(s, krows, stride=2), :],
                     (y * 2 + e) * 2 + s, ((y * 2 + e) * 2 + s) * blk, j * sub_q, hhi, hlo)
    total = total + gram(hhi[mine, :], hlo[mine, :], hhi[mine, :], hlo[mine, :])
    diag[...] = total
    cp = remote(diag.at[pl.ds((1 - c) * d_half, d_half)], dcore, dc_s, dc_r, partner)
    cp.wait()
    my_d = pl.ds(pl.multiple_of(c * d_half, d_half), d_half)
    dfull[lo, y, my_d, :] = diag[my_d, :] + dcore[...]
    my_diag = dfull.at[lo, y, my_d]
    dx = [remote(my_diag, my_diag, dx_s, dx_r, x_peer)]
    dys = [remote(my_diag, my_diag, dy_s.at[d], dy_r.at[d], (a, y_peer(d) * 2 + c)) for d in range(1, n_y)]

    offs = [(i, k) for i in range(n_y) for k in range(i)]
    for j in range(n_sub):
        for cp in tile_copies[j]:
            cp.wait()
        for d in range(1, n_y):
            for e in range(2):
                for s in range(2):
                    src = y_peer(d) * 2 + e
                    half(lambda q: rx[src, j * sub_q + q, pl.ds(s, krows, stride=2), :],
                         src * 2 + s, (src * 2 + s) * blk, j * sub_q, hhi, hlo)
        at = slice(j * sub_q * n_orb, (j + 1) * sub_q * n_orb)
        for b, (i, k) in enumerate(offs):
            ri, rk = slice(i * side, (i + 1) * side), slice(k * side, (k + 1) * side)
            val = gram(hhi[ri, at], hlo[ri, at], hhi[rk, at], hlo[rk, at])
            if j:
                val = val + off[b * side:(b + 1) * side, :]
            off[b * side:(b + 1) * side, :] = val
    cp = remote(off.at[pl.ds((1 - c) * o_half, o_half)], ocore, oc_s, oc_r, partner)
    cp.wait()
    opair[...] = off[pl.ds(pl.multiple_of(c * o_half, piece), o_half), :] + ocore[...]
    oys = []
    for p in range(PIECES):
        at = pl.ds(p * piece, piece)
        oys.append([remote(opair.at[at], oin.at[d - 1, at], oy_s.at[p, d - 1], oy_r.at[p, d - 1],
                           (a, y_peer(d) * 2 + c)) for d in range(1, n_y)])
    dfs = []
    for d in range(1, n_y):
        dys[d - 1].wait_recv()
        got = dfull.at[lo, y_peer(n_y - d), my_d]
        dfs.append(remote(got, got, df_s.at[d], df_r.at[d], x_peer))
    oxs, ops = [], []
    for p in range(PIECES):
        val = opair[p * piece:(p + 1) * piece, :]
        for d in range(1, n_y):
            oys[p][d - 1].wait()
            val = val + oin[d - 1, p * piece:(p + 1) * piece, :]
        at = pl.ds(pl.multiple_of(c * o_half + p * piece, piece), piece)
        ofull[lo, at, :] = val
        ref = ofull.at[lo, at]
        oxs.append(remote(ref, ref, ox_s.at[p], ox_r.at[p], x_peer))
        ops.append(remote(ref, ref, op_s.at[p], op_r.at[p], partner))
    for cp in dx + dfs:
        cp.wait()
    for cp in dys:
        cp.wait_send()
    idx_copy.wait()
    half_d = dfull.at[:, :, my_d]
    cp = remote(half_d, half_d, dd_s, dd_r, partner)

    out_rows, out_cols = out.shape
    compact = n_slots * blk
    col_pos = lax.broadcasted_iota(jnp.int32, (out_cols, compact), 0) + o * out_cols
    row_i = lax.broadcasted_iota(jnp.int32, (n_hi * out_rows, compact), 0)
    row_pos = (row_i // out_rows * 2 + lo) * out_rows + lax.rem(row_i, out_rows)
    picks = []
    for l in range(2):
        where = jnp.concatenate([ids[l, s, 2:3, :] for s in range(n_occ)], axis=1)
        picks.append([(pos == where).astype(jnp.float32).astype(jnp.bfloat16) for pos in (col_pos, row_pos)])

    def spread(acc, l, i, t):
        for e in split(t):
            v = dot(picks[l][1][:, i * side:(i + 1) * side], e, NN)
            acc = v if acc is None else acc + v
        return acc

    cp.wait()
    acc = None
    for l in range(2):
        for i in range(n_y):
            dh, dl = split(dfull[l, i])
            cols = picks[l][0][:, i * side:(i + 1) * side]
            acc = spread(acc, l, i, dot(dh, cols, NT) + dot(dl, cols, NT))
    fwd = []
    for p in range(PIECES):
        oxs[p].wait()
        ref = ofull.at[1 - lo, pl.ds(pl.multiple_of(c * o_half + p * piece, piece), piece)]
        fwd.append(remote(ref, ref, of_s.at[p], of_r.at[p], partner))
    for cp in ops + fwd:
        cp.wait()
    for l in range(2):
        t = [None] * n_y
        for b, (i, k) in enumerate(offs):
            for e in split(ofull[l, b * side:(b + 1) * side, :]):
                vi = dot(e, picks[l][0][:, k * side:(k + 1) * side], NT)
                vk = dot(e, picks[l][0][:, i * side:(i + 1) * side], (((0,), (1,)), ((), ())))
                t[i] = vi if t[i] is None else t[i] + vi
                t[k] = vk if t[k] is None else t[k] + vk
        for i in range(n_y):
            acc = spread(acc, l, i, t[i])
    for h in range(n_hi):
        dense[h] = acc[h * out_rows:(h + 1) * out_rows, :]
    zs = []
    for d in range(1, n_hi):
        zs.append(remote(dense.at[lax.rem(hi_a + d, n_hi)], z_in.at[d - 1],
                         z_s.at[d - 1], z_r.at[d - 1], z_peer(d)))
    result = dense[hi_a]
    for d in range(1, n_hi):
        zs[d - 1].wait()
        result = result + z_in[d - 1]
    out[...] = result


def per_device(n_aux, n_occ, blocks, pair_list, pair_count, orbitals):
    n_q, slots, area = blocks.shape
    n_orb, nbf = orbitals.shape
    krows = area // LANES
    blk = 2 * krows
    tiles = blocks.reshape(n_q, slots, krows, LANES).transpose(0, 2, 1, 3).reshape(n_q, krows * slots, LANES)
    own_q = n_q // n_occ
    n_sub = 3
    sub_k = own_q // n_sub * n_orb
    compact = slots * n_occ * blk
    side = 2 * slots * blk
    n_y, n_hi = n_occ // 2, n_aux // 2
    off_rows = n_y * (n_y - 1) // 2 * side
    out_rows, out_cols = nbf // n_aux, nbf // n_occ
    f32, bf16, dma, vmem = jnp.float32, jnp.bfloat16, pltpu.SemaphoreType.DMA, pltpu.VMEM
    sems = [(n_y,)] + [(n_sub, n_occ)] * 2 + [(n_y,)] * 2 + [(n_occ - 1,)] * 2 + [()] * 6 + [(n_y,)] * 4
    sems += [()] * 4 + [(PIECES, n_y - 1)] * 2 + [(PIECES,)] * 6 + [(n_hi - 1,)] * 2
    return pl.pallas_call(
        functools.partial(kernel, n_aux, n_occ, n_sub),
        name="exchange",
        out_shape=jax.ShapeDtypeStruct((out_rows, out_cols), f32),
        in_specs=[pl.BlockSpec(memory_space=pl.ANY)] + [pl.BlockSpec(memory_space=pltpu.SMEM)] * 2
        + [pl.BlockSpec(memory_space=vmem)],
        out_specs=pl.BlockSpec(memory_space=vmem),
        scratch_shapes=[
            vmem((n_occ, own_q, krows * slots, LANES), f32),
            vmem((2, n_y - 1, own_q, krows * slots, LANES), f32),
            vmem((2, n_occ, 8, LANES), jnp.int32),
            vmem((slots * n_occ, 2 * n_orb, LANES), bf16),
            vmem((slots * n_occ, 2 * n_orb, LANES), bf16),
            vmem((compact, own_q * n_orb), bf16),
            vmem((compact, own_q * n_orb), bf16),
            vmem((side, sub_k), bf16),
            vmem((side, sub_k), bf16),
            vmem((side, side), f32),
            vmem((side // 2, side), f32),
            vmem((2, n_y, side, side), f32),
            vmem((off_rows, side), f32),
            vmem((off_rows // 2, side), f32),
            vmem((off_rows // 2, side), f32),
            vmem((n_y - 1, off_rows // 2, side), f32),
            vmem((2, off_rows, side), f32),
            vmem((n_hi, out_rows, out_cols), f32),
            vmem((n_hi - 1, out_rows, out_cols), f32),
        ] + [dma(s) for s in sems],
        compiler_params=pltpu.CompilerParams(collective_id=0, has_side_effects=True),
    )(tiles, pair_list, pair_count, orbitals)


def solution(mesh):
    body = functools.partial(per_device, mesh.shape["aux"], mesh.shape["occ"])
    in_specs = (P("aux", "occ", None), P("aux", "occ", None), P("aux"), P())
    return jax.shard_map(body, mesh=mesh, in_specs=in_specs, out_specs=P("aux", "occ"), check_vma=False)
```

```python
import functools
import math

import jax
import jax.numpy as jnp
from jax import lax
from jax.experimental import pallas as pl
from jax.experimental.pallas import tpu as pltpu
from jax.sharding import PartitionSpec as P

LANES = 128
PIECES = 2
MESH = pl.DeviceIdType.MESH
NT = (((1,), (1,)), ((), ()))
NN = (((1,), (0,)), ((), ()))


def dot(a, b, dims):
    return lax.dot_general(a, b, dims, preferred_element_type=jnp.float32)


def split(x):
    hi = x.astype(jnp.bfloat16)
    return hi, (x - hi.astype(jnp.float32)).astype(jnp.bfloat16)


def kernel(n_aux, n_occ, n_sub, tiles, pairs_hbm, count_in, orb_hbm, out, pairs_in, orb, rx, rxd, ids, whi, wlo, hhi, hlo,
           dhi, dlo, diag, dcore, dfull, off, ocore, opair, oin, ofull, dense, z_in,
           in_s, local_s, tile_s, tile_r, quart_s, quart_r, ids_s, ids_r, idx_s, idx_r, dc_s, dc_r,
           dx_s, dx_r, dy_s, dy_r, df_s, df_r, dd_s, dd_r, oc_s, oc_r, oy_s, oy_r, ox_s, ox_r,
           op_s, op_r, of_s, of_r, z_s, z_r):
    a, o = lax.axis_index("aux"), lax.axis_index("occ")
    n_y, n_hi = n_occ // 2, n_aux // 2
    y, c = o // 2, lax.rem(o, 2)
    hi_a, lo = a // 2, lax.rem(a, 2)
    own_q = tiles.shape[0] // n_occ
    sub_q = own_q // n_sub
    krows = tiles.shape[1] // 2
    blk = 2 * krows
    side = 4 * blk
    n_slots = 2 * n_occ
    n_off = n_y * (n_y - 1) // 2
    d_half, o_half = side // 2, n_off * side // 2
    piece = o_half // PIECES
    nbf, n_orb = orb.shape[1], orb.shape[0]

    def y_peer(d):
        return lax.rem(y + d, n_y)

    peers = [(d, e) for d in range(1, n_y) for e in (0, 1)] + [(0, 1)]

    def occ_peer(d, e):
        return y_peer(d) * 2 + (c if e == 0 else 1 - c)

    partner = (a, occ_peer(0, 1))
    x_peer = (a + 1 - 2 * lo, o)

    def z_peer(d):
        return (lax.rem(hi_a + d, n_hi) * 2 + lo, o)

    barrier = pltpu.get_barrier_semaphore()
    greet = [(a, occ_peer(*d)) for d in peers] + [x_peer] + [z_peer(d) for d in range(1, n_hi)]
    for dev in greet:
        pl.semaphore_signal(barrier, inc=1, device_id=dev, device_id_type=MESH)

    def local(src, dst, s):
        cp = pltpu.make_async_copy(src, dst, s)
        cp.start()
        return cp

    def quarter(index):
        return tiles.at[pl.ds(index * own_q, own_q)]

    inputs = [local(src, dst, in_s.at[n]) for n, (src, dst) in enumerate(
        ((pairs_hbm, pairs_in), (orb_hbm, orb)))]
    locals_ = [local(quarter(o), rx.at[o], local_s.at[0])]
    for d in range(1, n_y):
        locals_.append(local(quarter(y_peer(d) * 2 + c), rxd.at[c, d - 1], local_s.at[d]))
    pl.semaphore_wait(barrier, len(greet))

    def remote(src, dst, s, r, dev):
        cp = pltpu.make_async_remote_copy(
            src_ref=src, dst_ref=dst, send_sem=s, recv_sem=r, device_id=dev, device_id_type=MESH
        )
        cp.start()
        return cp

    def sub_tiles(j, d, e):
        peer = occ_peer(d, e)
        n = d * 2 + e
        return remote(tiles.at[pl.ds(peer * own_q + j * sub_q, sub_q)], rx.at[o, pl.ds(j * sub_q, sub_q)],
                      tile_s.at[j, n], tile_r.at[j, n], (a, peer))

    def tiles_of(j):
        return [sub_tiles(j, d, e) for d in range(1, n_y) for e in (0, 1)]

    tile_copies = [tiles_of(0)]
    quarters = []
    inputs[0].wait()
    lane1 = lax.broadcasted_iota(jnp.int32, (8, LANES), 1)
    row1 = lax.broadcasted_iota(jnp.int32, (8, LANES), 0)
    within = lax.rem(lane1, blk)
    place = lax.rem(within, krows) * 2 + within // krows
    live = [jnp.where(o * 2 + s < count_in[0], pairs_in[0, s, 0] * blk, -nbf - blk) for s in range(2)]
    cols = jnp.where(row1 == 0, pairs_in[0, 0, 1], pairs_in[0, 1, 1]) * blk + within
    ids[lo, o] = jnp.where(row1 < 2, cols, jnp.where(lane1 < blk, live[0], live[1]) + place)
    id_copies = []
    for n, d in enumerate(peers):
        id_copies.append(remote(ids.at[lo, o], ids.at[lo, o], ids_s.at[n], ids_r.at[n], (a, occ_peer(*d))))
    for d in range(1, n_y):
        quarters.append(remote(quarter(y_peer(d) * 2 + 1 - c), rxd.at[c, d - 1],
                               quart_s.at[d], quart_r.at[d], partner))
    quarters.append(remote(quarter(o + 1 - 2 * c), rx.at[o], quart_s.at[0], quart_r.at[0], partner))
    for j in range(1, n_sub):
        tile_copies.append(tiles_of(j))
    inputs[1].wait()
    orb_hi, orb_lo = split(orb[...])
    row_pos = lax.broadcasted_iota(jnp.int32, (nbf, LANES), 0)
    lane = lax.broadcasted_iota(jnp.int32, (n_orb, LANES), 1)
    def weights(src):
        for s in range(2):
            sel = (row_pos == ids[lo, src, pl.ds(s, 1), :]).astype(jnp.float32).astype(jnp.bfloat16)
            for orb_part, copies, dst in ((orb_hi, 2, whi), (orb_lo, 1, wlo)):
                w = dot(orb_part, sel, NN)
                for p in range(2):
                    keep = lane < blk if p == 0 else lane >= blk
                    w_p = jnp.where(keep, w, 0.0).astype(jnp.bfloat16)
                    for n in range(copies):
                        dst[src * 2 + s, p * n_orb:(p + 1) * n_orb, n * LANES:(n + 1) * LANES] = w_p

    id_copies[-1].wait()
    for e in range(2):
        weights(y * 2 + e)

    def half(load, slot, row0, q0, hi_ref, lo_ref):
        rows = jnp.concatenate([load(q) for q in range(sub_q)], axis=0)
        bh, bl = split(rows)
        wh, wl = whi[slot], wlo[slot]
        res = dot(jnp.concatenate([bh, bl], axis=1), wh, NT) + dot(bh, wl, NT)
        for q in range(sub_q):
            for p in range(2):
                ph, pl_ = split(res[q * krows:(q + 1) * krows, p * n_orb:(p + 1) * n_orb])
                at = pl.ds(pl.multiple_of(row0 + p * krows, krows), krows)
                lanes = slice((q0 + q) * n_orb, (q0 + q + 1) * n_orb)
                hi_ref[at, lanes] = ph
                lo_ref[at, lanes] = pl_

    def gram(hi_i, lo_i, hi_k, lo_k):
        return dot(hi_i, hi_k, NT) + dot(hi_i, lo_k, NT) + dot(lo_i, hi_k, NT)

    for cp in locals_ + quarters:
        cp.wait()
    total = None
    for d in range(1, n_y):
        for j in range(n_sub):
            for e in range(2):
                for s in range(2):
                    half(lambda q: rxd[e, d - 1, j * sub_q + q, pl.ds(s, krows, stride=2), :],
                         (y * 2 + e) * 2 + s, (e * 2 + s) * blk, 0, dhi, dlo)
            val = gram(dhi[...], dlo[...], dhi[...], dlo[...])
            total = val if total is None else total + val
    mine = pl.ds(pl.multiple_of(y * side, side), side)
    for j in range(n_sub):
        for e in range(2):
            for s in range(2):
                half(lambda q: rx[y * 2 + e, j * sub_q + q, pl.ds(s, krows, stride=2), :],
                     (y * 2 + e) * 2 + s, ((y * 2 + e) * 2 + s) * blk, j * sub_q, hhi, hlo)
    total = total + gram(hhi[mine, :], hlo[mine, :], hhi[mine, :], hlo[mine, :])
    diag[...] = total
    cp = remote(diag.at[pl.ds((1 - c) * d_half, d_half)], dcore, dc_s, dc_r, partner)
    cp.wait()
    my_d = pl.ds(pl.multiple_of(c * d_half, d_half), d_half)
    dfull[lo, y, my_d, :] = diag[my_d, :] + dcore[...]
    my_diag = dfull.at[lo, y, my_d]
    dx = [remote(my_diag, my_diag, dx_s, dx_r, x_peer)]
    dys = [remote(my_diag, my_diag, dy_s.at[d], dy_r.at[d], (a, y_peer(d) * 2 + c)) for d in range(1, n_y)]

    for cp in id_copies[:-1]:
        cp.wait()
    idx_copy = remote(ids.at[lo], ids.at[lo], idx_s, idx_r, x_peer)
    for d in range(1, n_y):
        for e in range(2):
            weights(y_peer(d) * 2 + e)
    offs = [(i, k) for i in range(n_y) for k in range(i)]
    for j in range(n_sub):
        for cp in tile_copies[j]:
            cp.wait()
        for d in range(1, n_y):
            for e in range(2):
                for s in range(2):
                    src = y_peer(d) * 2 + e
                    half(lambda q: rx[src, j * sub_q + q, pl.ds(s, krows, stride=2), :],
                         src * 2 + s, (src * 2 + s) * blk, j * sub_q, hhi, hlo)
        at = slice(j * sub_q * n_orb, (j + 1) * sub_q * n_orb)
        for b, (i, k) in enumerate(offs):
            ri, rk = slice(i * side, (i + 1) * side), slice(k * side, (k + 1) * side)
            val = gram(hhi[ri, at], hlo[ri, at], hhi[rk, at], hlo[rk, at])
            if j:
                val = val + off[b * side:(b + 1) * side, :]
            off[b * side:(b + 1) * side, :] = val
    cp = remote(off.at[pl.ds((1 - c) * o_half, o_half)], ocore, oc_s, oc_r, partner)
    cp.wait()
    opair[...] = off[pl.ds(pl.multiple_of(c * o_half, piece), o_half), :] + ocore[...]
    oys = []
    for p in range(PIECES):
        at = pl.ds(p * piece, piece)
        oys.append([remote(opair.at[at], oin.at[d - 1, at], oy_s.at[p, d - 1], oy_r.at[p, d - 1],
                           (a, y_peer(d) * 2 + c)) for d in range(1, n_y)])
    dfs = []
    for d in range(1, n_y):
        dys[d - 1].wait_recv()
        got = dfull.at[lo, y_peer(n_y - d), my_d]
        dfs.append(remote(got, got, df_s.at[d], df_r.at[d], x_peer))
    oxs, ops = [], []
    for p in range(PIECES):
        val = opair[p * piece:(p + 1) * piece, :]
        for d in range(1, n_y):
            oys[p][d - 1].wait()
            val = val + oin[d - 1, p * piece:(p + 1) * piece, :]
        at = pl.ds(pl.multiple_of(c * o_half + p * piece, piece), piece)
        ofull[lo, at, :] = val
        ref = ofull.at[lo, at]
        oxs.append(remote(ref, ref, ox_s.at[p], ox_r.at[p], x_peer))
        ops.append(remote(ref, ref, op_s.at[p], op_r.at[p], partner))
    for cp in dx + dfs:
        cp.wait()
    for cp in dys:
        cp.wait_send()
    idx_copy.wait()
    half_d = dfull.at[:, :, my_d]
    cp = remote(half_d, half_d, dd_s, dd_r, partner)

    out_rows, out_cols = out.shape[1:]
    compact = n_slots * blk
    col_pos = lax.broadcasted_iota(jnp.int32, (out_cols, compact), 0) + o * out_cols
    row_i = lax.broadcasted_iota(jnp.int32, (n_hi * out_rows, compact), 0)
    row_h = lax.rem(row_i // out_rows + 1 + hi_a, n_hi)
    row_pos = (row_h * 2 + lo) * out_rows + lax.rem(row_i, out_rows)
    picks = []
    for l in range(2):
        where = jnp.concatenate([ids[l, s, 2:3, :] for s in range(n_occ)], axis=1)
        picks.append([(pos == where).astype(jnp.float32).astype(jnp.bfloat16) for pos in (col_pos, row_pos)])

    def spread(acc, l, i, t):
        for e in split(t):
            v = dot(picks[l][1][:, i * side:(i + 1) * side], e, NN)
            acc = v if acc is None else acc + v
        return acc

    cp.wait()
    acc = None
    for l in range(2):
        for i in range(n_y):
            dh, dl = split(dfull[l, i])
            cols = picks[l][0][:, i * side:(i + 1) * side]
            acc = spread(acc, l, i, dot(dh, cols, NT) + dot(dl, cols, NT))
    fwd = []
    for p in range(PIECES):
        oxs[p].wait()
        ref = ofull.at[1 - lo, pl.ds(pl.multiple_of(c * o_half + p * piece, piece), piece)]
        fwd.append(remote(ref, ref, of_s.at[p], of_r.at[p], partner))
    for cp in ops + fwd:
        cp.wait()
    parts = []
    for l in range(2):
        t = [None] * n_y
        for b, (i, k) in enumerate(offs):
            for e in split(ofull[l, b * side:(b + 1) * side, :]):
                vi = dot(e, picks[l][0][:, k * side:(k + 1) * side], NT)
                vk = dot(e, picks[l][0][:, i * side:(i + 1) * side], (((0,), (1,)), ((), ())))
                t[i] = vi if t[i] is None else t[i] + vi
                t[k] = vk if t[k] is None else t[k] + vk
        parts.append([split(v) for v in t])
    zs = []
    for g in range(n_hi // 2):
        rows = slice(2 * g * out_rows, 2 * (g + 1) * out_rows)
        v = acc[rows, :]
        for l in range(2):
            for i in range(n_y):
                for e in parts[l][i]:
                    v = v + dot(picks[l][1][rows, i * side:(i + 1) * side], e, NN)
        for n in range(2):
            d = 2 * g + n + 1
            if d < n_hi:
                dense[d - 1] = v[n * out_rows:(n + 1) * out_rows, :]
                zs.append(remote(dense.at[d - 1], z_in.at[d - 1], z_s.at[d - 1], z_r.at[d - 1], z_peer(d)))
            else:
                out[0] = v[n * out_rows:(n + 1) * out_rows, :]
    result = None
    for d in range(1, n_hi):
        zs[d - 1].wait()
        result = z_in[d - 1] if result is None else result + z_in[d - 1]
    out[1] = result


def per_device(n_aux, n_occ, blocks, pair_list, pair_count, orbitals):
    n_q, slots, area = blocks.shape
    n_orb, nbf = orbitals.shape
    krows = area // LANES
    blk = 2 * krows
    tiles = blocks.reshape(n_q, slots, krows, LANES).transpose(0, 2, 1, 3).reshape(n_q, krows * slots, LANES)
    own_q = n_q // n_occ
    n_sub = math.gcd(own_q, 6)
    sub_k = own_q // n_sub * n_orb
    compact = slots * n_occ * blk
    side = 2 * slots * blk
    n_y, n_hi = n_occ // 2, n_aux // 2
    off_rows = n_y * (n_y - 1) // 2 * side
    out_rows, out_cols = nbf // n_aux, nbf // n_occ
    f32, bf16, dma, vmem = jnp.float32, jnp.bfloat16, pltpu.SemaphoreType.DMA, pltpu.VMEM
    sems = [(2,), (n_y,)] + [(n_sub, n_occ)] * 2 + [(n_y,)] * 2 + [(n_occ - 1,)] * 2 + [()] * 6 + [(n_y,)] * 4
    sems += [()] * 4 + [(PIECES, n_y - 1)] * 2 + [(PIECES,)] * 6 + [(n_hi - 1,)] * 2
    sums = pl.pallas_call(
        functools.partial(kernel, n_aux, n_occ, n_sub),
        name="exchange",
        out_shape=jax.ShapeDtypeStruct((2, out_rows, out_cols), f32),
        in_specs=[pl.BlockSpec(memory_space=space) for space in (pl.ANY, pl.ANY, pltpu.SMEM, pl.ANY)],
        out_specs=pl.BlockSpec(memory_space=vmem),
        scratch_shapes=[
            pltpu.SMEM(pair_list.shape, jnp.int32),
            vmem(orbitals.shape, f32),
            vmem((n_occ, own_q, krows * slots, LANES), f32),
            vmem((2, n_y - 1, own_q, krows * slots, LANES), f32),
            vmem((2, n_occ, 8, LANES), jnp.int32),
            vmem((slots * n_occ, 2 * n_orb, 2 * LANES), bf16),
            vmem((slots * n_occ, 2 * n_orb, LANES), bf16),
            vmem((compact, own_q * n_orb), bf16),
            vmem((compact, own_q * n_orb), bf16),
            vmem((side, sub_k), bf16),
            vmem((side, sub_k), bf16),
            vmem((side, side), f32),
            vmem((side // 2, side), f32),
            vmem((2, n_y, side, side), f32),
            vmem((off_rows, side), f32),
            vmem((off_rows // 2, side), f32),
            vmem((off_rows // 2, side), f32),
            vmem((n_y - 1, off_rows // 2, side), f32),
            vmem((2, off_rows, side), f32),
            vmem((n_hi - 1, out_rows, out_cols), f32),
            vmem((n_hi - 1, out_rows, out_cols), f32),
        ] + [dma(s) for s in sems],
        compiler_params=pltpu.CompilerParams(collective_id=0, has_side_effects=True),
    )(tiles, pair_list, pair_count, orbitals)
    return sums[0] + sums[1]


def solution(mesh):
    body = functools.partial(per_device, mesh.shape["aux"], mesh.shape["occ"])
    in_specs = (P("aux", "occ", None), P("aux", "occ", None), P("aux"), P())
    return jax.shard_map(body, mesh=mesh, in_specs=in_specs, out_specs=P("aux", "occ"), check_vma=False)
```
